32 devices in a mesh: groups: 2 (over y), tm: 4 (over z), mp: 2 (over x), sub: 2 (over core).
Axes of the slice: x: 2, y: 2, z: 4, core: 2. Of those that a mesh axis runs over, the one named last changes fastest.
Arguments:
- events: bfloat16 [16384, 768], P(('groups', 'tm', 'sub')), parts along dimension 0, may hold values from -6 to 6
- w_gate: bfloat16 [768, 1536], P(None, 'mp'), may hold values from -0.21875 to 0.21875
- w_inner: bfloat16 [768, 1536], P(None, 'mp'), may hold values from -0.21875 to 0.21875
- w_bc: bfloat16 [768, 256], replicated, may hold values from -0.21875 to 0.21875
- w_step: bfloat16 [768, 24], P(None, 'mp'), may hold values from -0.21875 to 0.21875
- step_bias: float32 [24], P('mp'), may hold values from -3 to 1
- log_decay: float32 [24, 16384], P('mp', ('groups', 'tm', 'sub')), parts along dimension 1, may hold values from -1 to 0
- norm_gain: float32 [1536], P('mp'), may hold values from 0.1 to 1.9
- w_out: bfloat16 [1536, 768], P('mp'), may hold values from -0.15625 to 0.15625
- mix_gain: float32 [768], replicated, may hold values from 0.1 to 1.9
- port: int32 [16384], P(('groups', 'tm', 'sub')), parts along dimension 0, may hold values from 0 to 15, as said below
- port_shard: int32 [32], P('groups'), parts along dimension 0, may hold values from 0 to 3, as said below
- w_up: bfloat16 [4, 768, 1536], P('tm', None, 'mp'), may hold values from -0.21875 to 0.21875
- b_up: float32 [4, 1536], P('tm', 'mp'), may hold values from -6 to 6
- w_down: bfloat16 [4, 1536, 768], P('tm', 'mp'), may hold values from -0.15625 to 0.15625
Outputs:
- readout: bfloat16 [16384, 768], P(('groups', 'tm', 'sub'), 'mp'), parts along dimension 0
The draws below stay inside these ranges and needn't reach their ends.
There are 2 independent parts, one for each index of `groups`. The reference program is written for one: setup_inputs(seed, part) draws one part's arguments, and reference() takes and returns one part's arrays. A program takes and returns all parts, laid end to end along the dimension named above; an argument that names none is the same for every part. Nothing has to cross between parts.
Inputs may be any that keep to these rules, and one draw needn't show every extreme that they name: Of the 1024 events of one device (aligned blocks of the trace, in order over tm and sub), exactly 512 belong to one port group, the same group for all devices of a trace and drawn per trace, and the rest are spread as evenly as possible over the other groups, so no device has more than 512 events of one group. Within a group, some ports are more frequent than others. `port_shard`: each port group owns exactly 4 ports.
All inputs are finite; a program needn't handle non-finite values.
Results may differ from the reference program's by a relative error of at most 0.02.
Values may be sent and summed in bfloat16 or wider, within the bound.
A program may use at most 64 MiB of HBM per device.

```python
import jax
import jax.numpy as jnp
from jax import lax

MODEL_WIDTH = 768
ATTENTION_LANES = 24
HEAD_DIM = 64
INNER = 1536
NSTATE = 128
READOUT_UNITS = 1536
BLOCK = 256
PORTS_SHARD = 4
TOK_DEV = 1024
LOGGED_ARRIVALS = 8192
CAP = 512
PORTS = 16
PORT_GROUPS = 4
N_TM = 4
N_MP = 2
N_SUB = 2


spike_total = 3


def port_ranking(key):
    return jax.random.permutation(jax.random.fold_in(key, 7), PORTS)


def draw_port_shard(key, part):
    return (port_ranking(key) % N_TM).astype(jnp.int32)


def draw_port(key, part):
    ranking_table = port_ranking(key)
    port_owner = jnp.argsort(ranking_table)
    blocks = LOGGED_ARRIVALS // TOK_DEV
    hottest = jax.random.randint(jax.random.fold_in(key, 8), (), 0, N_TM)
    random_seed_stream = jax.random.split(jax.random.fold_in(key, 9), blocks)
    ranking = jax.vmap(lambda block_key: jax.random.permutation(block_key, TOK_DEV))(random_seed_stream)
    offsets = jax.random.randint(jax.random.fold_in(key, 10), (blocks, 1), 0, N_TM - 1)
    others = (hottest + 1 + (ranking - CAP + offsets) % (N_TM - 1)) % N_TM
    dest_shard = jnp.where(ranking < CAP, hottest, others)
    first_draw = jax.random.randint(jax.random.fold_in(key, 11), (blocks, TOK_DEV), 0, PORTS_SHARD)
    second_draw = jax.random.randint(jax.random.fold_in(key, 12), (blocks, TOK_DEV), 0, PORTS_SHARD)
    pick_rank = jnp.minimum(first_draw, second_draw)
    return port_owner[dest_shard + N_TM * pick_rank].reshape(LOGGED_ARRIVALS).astype(jnp.int32)


def draw_log_decay(key, part):
    random_seed_stream = [jax.random.fold_in(key, 20 + number) for number in range(8)]
    fast_share = 0.5
    fast_head = jax.random.uniform(random_seed_stream[0], (ATTENTION_LANES, 1)) < fast_share
    fast_rate = jnp.exp(jax.random.uniform(random_seed_stream[1], (ATTENTION_LANES, 1), minval=jnp.log(1.0 / 50.0), maxval=jnp.log(1.0 / 30.0)))
    slow_rate = jnp.exp(jax.random.uniform(random_seed_stream[2], (ATTENTION_LANES, 1), minval=jnp.log(0.05), maxval=jnp.log(0.3))) / LOGGED_ARRIVALS
    fading_speed = jnp.where(fast_head, fast_rate, slow_rate)
    segment_multiplier = jnp.exp(jax.random.uniform(random_seed_stream[3], (ATTENTION_LANES, LOGGED_ARRIVALS // BLOCK, 1), minval=-0.5, maxval=0.5))
    segment_multiplier = jnp.broadcast_to(segment_multiplier, (ATTENTION_LANES, LOGGED_ARRIVALS // BLOCK, BLOCK)).reshape(ATTENTION_LANES, LOGGED_ARRIVALS)
    arrival_jitter = jax.random.uniform(random_seed_stream[4], (ATTENTION_LANES, LOGGED_ARRIVALS), minval=0.5, maxval=1.5)
    arrival_positions = jax.random.randint(random_seed_stream[5], (spike_total,), 0, LOGGED_ARRIVALS)
    spike_arrivals = jnp.any(jnp.arange(LOGGED_ARRIVALS)[None, :] == arrival_positions[:, None], axis=0)
    spike_length = jnp.log(jax.random.uniform(random_seed_stream[6], (ATTENTION_LANES, LOGGED_ARRIVALS), minval=0.55, maxval=0.8))
    payload_entries = -fading_speed * segment_multiplier * arrival_jitter + jnp.where(spike_arrivals[None, :], spike_length, 0.0)
    return payload_entries.astype(jnp.float32)


def steps_of(stream_key, dims, cuts, least, largest):
    def one(dim, shards_of):
        heights = jax.random.uniform(jax.random.fold_in(jax.random.fold_in(stream_key, 6), dim), (shards_of,), jnp.float32, least / len(cuts), largest / len(cuts))
        return jnp.repeat(jnp.exp(heights), dims[dim] // shards_of).reshape((-1,) + (1,) * (len(dims) - dim - 1))

    level = one(*cuts[0])
    for cut in cuts[1:]:
        level = level * one(*cut)
    return level


def centred(stream_key, extent, scale, bound, pieces=(), held_as=jnp.bfloat16):
    values = scale * jax.random.normal(stream_key, extent, jnp.float32)
    if pieces:
        values = values * steps_of(stream_key, extent, pieces, -0.22, 0.18)
    return jnp.clip(values, -bound, bound).astype(held_as)


def setup_inputs(seed: int = 0, part: int = 0) -> dict:
    keys = jax.random.split(jax.random.key(seed), 16)
    part_keys = jax.random.split(jax.random.fold_in(keys[15], part), 16)
    return {
        "events": centred(part_keys[0], (LOGGED_ARRIVALS, MODEL_WIDTH), 1.0, 6.0, ((0, 8),)),
        "w_gate": centred(keys[1], (MODEL_WIDTH, INNER), MODEL_WIDTH ** -0.5, 0.21875, ((1, 2),)),
        "w_inner": centred(keys[2], (MODEL_WIDTH, INNER), MODEL_WIDTH ** -0.5, 0.21875, ((1, 2),)),
        "w_bc": centred(keys[3], (MODEL_WIDTH, 2 * NSTATE), MODEL_WIDTH ** -0.5, 0.21875),
        "w_step": centred(keys[4], (MODEL_WIDTH, ATTENTION_LANES), MODEL_WIDTH ** -0.5, 0.21875, ((1, 2),)),
        "step_bias": jnp.clip(-3.0 + 4.0 * jax.random.uniform(keys[5], (ATTENTION_LANES,), jnp.float32) ** steps_of(keys[5], (ATTENTION_LANES,), ((0, 2),), -0.2, 0.2), -3.0, 1.0),
        "log_decay": draw_log_decay(jax.random.fold_in(jax.random.fold_in(keys[15], part), 71), part),
        "norm_gain": jnp.clip(1.0 + 0.18 * jax.random.normal(keys[7], (INNER,), jnp.float32), 0.1, 1.9),
        "w_out": centred(keys[8], (INNER, MODEL_WIDTH), INNER ** -0.5, 0.15625, ((0, 2),)),
        "mix_gain": jnp.clip(1.0 + 0.18 * jax.random.normal(keys[9], (MODEL_WIDTH,), jnp.float32), 0.1, 1.9),
        "port": draw_port(jax.random.fold_in(jax.random.fold_in(keys[15], part), 71), part),
        "port_shard": draw_port_shard(jax.random.fold_in(jax.random.fold_in(keys[15], part), 71), part),
        "w_up": centred(keys[12], (PORT_GROUPS, MODEL_WIDTH, READOUT_UNITS), MODEL_WIDTH ** -0.5, 0.21875, ((0, 4), (2, 2))),
        "b_up": centred(keys[13], (PORT_GROUPS, READOUT_UNITS), 1.0, 6.0, ((0, 4), (1, 2)), jnp.float32),
        "w_down": centred(keys[14], (PORT_GROUPS, READOUT_UNITS, MODEL_WIDTH), READOUT_UNITS ** -0.5, 0.15625, ((0, 4), (1, 2))),
    }


def scan_block(state, inputs):
    b_part, c_part, x_part, decay_part = inputs
    running = jnp.cumsum(decay_part, axis=1)
    causal_mask = jnp.arange(BLOCK)[:, None] >= jnp.arange(BLOCK)[None, :]
    spread = running[:, :, None] - running[:, None, :]
    weights = jnp.where(causal_mask[None], jnp.exp(jnp.where(causal_mask[None], spread, 0.0)), 0.0)
    affinity = jnp.dot(c_part, b_part.T, preferred_element_type=jnp.float32)
    x_float = x_part.astype(jnp.float32)
    within = jnp.einsum('hij,jhp->ihp', affinity[None] * weights, x_float, precision=lax.Precision.HIGHEST)
    c_float = c_part.astype(jnp.float32)
    carried = jnp.einsum('in,hi,hnp->ihp', c_float, jnp.exp(running), state, precision=lax.Precision.HIGHEST)
    to_end = jnp.exp(running[:, -1:] - running)
    fresh = jnp.einsum('jn,hj,jhp->hnp', b_part.astype(jnp.float32), to_end, x_float, precision=lax.Precision.HIGHEST)
    new_state = jnp.exp(running[:, -1])[:, None, None] * state + fresh
    return (new_state, within + carried)

def reference(events, w_gate, w_inner, w_bc, w_step, step_bias, log_decay, norm_gain, w_out, mix_gain, port, port_shard, w_up, b_up, w_down):
    gate_pre = jnp.dot(events, w_gate, preferred_element_type=jnp.float32)
    inner_pre = jnp.dot(events, w_inner, preferred_element_type=jnp.float32)
    bc_proj = jnp.dot(events, w_bc, preferred_element_type=jnp.float32).astype(jnp.bfloat16)
    step_size = jax.nn.softplus(jnp.dot(events, w_step, preferred_element_type=jnp.float32) + step_bias[None, :])
    scaled = (inner_pre.reshape(LOGGED_ARRIVALS, ATTENTION_LANES, HEAD_DIM) * step_size[:, :, None]).astype(jnp.bfloat16)
    blocks = LOGGED_ARRIVALS // BLOCK
    b_blocks = bc_proj[:, :NSTATE].reshape(blocks, BLOCK, NSTATE)
    c_blocks = bc_proj[:, NSTATE:].reshape(blocks, BLOCK, NSTATE)
    x_blocks = scaled.reshape(blocks, BLOCK, ATTENTION_LANES, HEAD_DIM)
    decay_blocks = log_decay.reshape(ATTENTION_LANES, blocks, BLOCK).transpose(1, 0, 2)
    start = jnp.zeros((ATTENTION_LANES, NSTATE, HEAD_DIM), jnp.float32)
    final_state, outputs = lax.scan(scan_block, start, (b_blocks, c_blocks, x_blocks, decay_blocks))
    ssm_out = outputs.reshape(LOGGED_ARRIVALS, ATTENTION_LANES, HEAD_DIM)
    gated = ssm_out * jax.nn.silu(gate_pre.reshape(LOGGED_ARRIVALS, ATTENTION_LANES, HEAD_DIM))
    square_mean = lax.optimization_barrier(jnp.mean(gated * gated, axis=2, keepdims=True))
    normed = (gated * lax.rsqrt(square_mean + 1e-05) * norm_gain.reshape(ATTENTION_LANES, HEAD_DIM)).reshape(LOGGED_ARRIVALS, INNER).astype(jnp.bfloat16)
    layer_out = jnp.dot(normed, w_out, preferred_element_type=jnp.float32)
    feature_mean = lax.optimization_barrier(jnp.mean(layer_out * layer_out, axis=1, keepdims=True))
    ready = (layer_out * lax.rsqrt(feature_mean + 1e-05) * mix_gain[None, :]).astype(jnp.bfloat16)
    target = port_shard[port]
    queue_buffer_size = N_SUB * N_TM * CAP

    def group_step(result, inputs):
        group_id, up_weight, up_bias, down_matrix = inputs
        member = target == group_id
        position = (jnp.cumsum(member.astype(jnp.int32)) - 1).astype(jnp.int32)
        placed = jnp.where(member, position, queue_buffer_size).astype(jnp.int32)
        gathered = jnp.zeros((queue_buffer_size, MODEL_WIDTH), jnp.bfloat16).at[placed].set(ready, mode='drop')
        hidden_units = jax.nn.gelu(jnp.dot(gathered, up_weight, preferred_element_type=jnp.float32) + up_bias[None, :], approximate=True).astype(jnp.bfloat16)
        trace_pieces = jnp.einsum('ojg,jgq->ojq', hidden_units.reshape(queue_buffer_size, N_MP, READOUT_UNITS // N_MP).astype(jnp.float32), down_matrix.reshape(N_MP, READOUT_UNITS // N_MP, MODEL_WIDTH).astype(jnp.float32))
        rounded = lax.optimization_barrier(trace_pieces.astype(jnp.bfloat16))
        summed = lax.optimization_barrier(jnp.sum(rounded.astype(jnp.float32), axis=1)).astype(jnp.bfloat16)
        picked = summed[jnp.clip(position, 0, queue_buffer_size - 1)]
        return (jnp.where(member[:, None], picked, result), None)
    readout, unused = lax.scan(group_step, jnp.zeros((LOGGED_ARRIVALS, MODEL_WIDTH), jnp.bfloat16), (jnp.arange(PORT_GROUPS, dtype=jnp.int32), w_up, b_up, w_down))
    return readout
```

```python
import functools

import jax
import jax.numpy as jnp
from jax import lax
from jax.experimental import pallas as pl
from jax.experimental.pallas import tpu as pltpu
from jax.sharding import PartitionSpec as P

SCAN = 128
ROWS = 256
CHUNKS = 4
BF = jnp.bfloat16
F32 = jnp.float32
HI = lax.Precision.HIGHEST
VMEM_BYTES = 60 * 2**20


def dot(a, b, precision=None):
    return jnp.dot(a, b, preferred_element_type=F32, precision=precision)


def iota(shape, dim):
    return lax.broadcasted_iota(jnp.int32, shape, dim)


def expander(heads, channels):
    head_dim = channels // heads
    return (iota((heads, channels), 1) // head_dim == iota((heads, channels), 0)).astype(BF)


def widen(v, spread):
    a = v.astype(BF)
    rest = v - a.astype(F32)
    b = rest.astype(BF)
    c = (rest - b.astype(F32)).astype(BF)
    return dot(a, spread) + dot(b, spread) + dot(c, spread)


def running_columns(decay, rows):
    lower = (iota((rows, rows), 0) >= iota((rows, rows), 1)).astype(F32)
    return lax.dot_general(
        lower, decay, (((1,), (1,)), ((), ())), precision=HI, preferred_element_type=F32
    )


def running_rows(decay, rows):
    upper = (iota((rows, rows), 0) <= iota((rows, rows), 1)).astype(F32)
    return dot(decay, upper, HI)


def project_kernel(
    ev, w_inner, w_bc, w_step, bias, decay, x_out, bc_out, run_out, start_out, end_out, state, total
):
    step = pl.program_id(0)
    nstate = state.shape[0]
    heads, channels = w_step.shape[1], w_inner.shape[1]

    @pl.when(step == 0)
    def _():
        state[...] = jnp.zeros_like(state)
        total[...] = jnp.zeros_like(total)

    e = ev[...]
    spread = expander(heads, channels)
    bc = dot(e, w_bc[...]).astype(BF)
    bc_out[...] = bc
    v = dot(e, w_step[...]) + bias[...]
    size = jnp.maximum(v, 0.0) + jnp.log1p(jnp.exp(-jnp.abs(v)))
    x = (dot(e, w_inner[...]) * widen(size, spread)).astype(BF)
    x_out[...] = x
    for b in range(ROWS // SCAN):
        rows = slice(b * SCAN, (b + 1) * SCAN)
        run = running_columns(decay[:, rows], SCAN)
        last = run[SCAN - 1 : SCAN, :]
        run_out[rows, :] = total[...] + run
        total[...] = total[...] + last
        to_end = dot(jnp.exp(last - run).astype(BF), spread)
        start_out[b] = state[...].astype(BF)
        fresh = lax.dot_general(
            bc[rows, :nstate],
            (x[rows, :].astype(F32) * to_end).astype(BF),
            (((0,), (0,)), ((), ())),
            preferred_element_type=F32,
        )
        kept = widen(jnp.broadcast_to(jnp.exp(last), (8, heads)), spread)[0:1, :]
        state[...] = kept * state[...] + fresh

    @pl.when(step == pl.num_programs(0) - 1)
    def _():
        end_out[0:nstate, :] = state[...].astype(BF)
        kept = widen(jnp.broadcast_to(jnp.exp(total[...]), (16, heads)), spread)
        high = kept.astype(BF).astype(F32)
        place = iota((16, channels), 0)
        end_out[nstate : nstate + 16, :] = jnp.where(
            place == 0, high, jnp.where(place == 1, kept - high, 0.0)
        ).astype(BF)


def within_kernel(ev, w_gate, x, bc, decay, start, y_out, gate_out):
    channels = x.shape[1]
    heads = decay.shape[0]
    head_dim = channels // heads
    nstate = bc.shape[1] // 2
    spread = expander(heads, channels)
    g = dot(ev[...], w_gate[...])
    gate_out[...] = (g / (1.0 + jnp.exp(-g))).astype(BF)
    causal = iota((SCAN, SCAN), 0) >= iota((SCAN, SCAN), 1)
    first = iota((SCAN, 2 * head_dim), 1) < head_dim
    for b in range(ROWS // SCAN):
        rows = slice(b * SCAN, (b + 1) * SCAN)
        run_c = running_columns(decay[:, rows], SCAN)
        run_r = running_rows(decay[:, rows], SCAN)
        b_in, c_out = bc[rows, :nstate], bc[rows, nstate:]
        affinity = lax.dot_general(
            c_out, b_in, (((1,), (1,)), ((), ())), preferred_element_type=F32
        )
        carried = dot(c_out, start[b]) * widen(jnp.exp(run_c), spread)
        for pair in range(heads // 2):
            cols = slice(pair * 2 * head_dim, (pair + 1) * 2 * head_dim)
            mixes = []
            for h in (2 * pair, 2 * pair + 1):
                gap = run_c[:, h : h + 1] - run_r[h : h + 1, :]
                mixes.append((affinity * jnp.exp(jnp.where(causal, gap, -1e30))).astype(BF))
            xp = x[rows, cols]
            zero = jnp.zeros_like(xp)
            blocks = jnp.concatenate([jnp.where(first, xp, zero), jnp.where(first, zero, xp)], axis=0)
            y_out[rows, cols] = dot(jnp.concatenate(mixes, axis=1), blocks) + carried[:, cols]


def out_kernel(y, gate, bc, run, carry, gain, w_out, part_out):
    channels = y.shape[1]
    heads = run.shape[1]
    head_dim = channels // heads
    nstate = carry.shape[0]
    spread = expander(heads, channels)
    ssm = y[...] + dot(bc[:, nstate:], carry[...]) * widen(jnp.exp(run[...]), spread)
    gated = ssm * gate[...].astype(F32)
    wide = 2 * head_dim
    ones = (iota((wide, wide), 0) // head_dim == iota((wide, wide), 1) // head_dim).astype(BF)
    sq = gated * gated
    high = sq.astype(BF)
    low = (sq - high.astype(F32)).astype(BF)
    pieces = []
    for pair in range(heads // 2):
        cols = slice(pair * wide, (pair + 1) * wide)
        mean = (dot(high[:, cols], ones) + dot(low[:, cols], ones)) * (1.0 / head_dim)
        pieces.append((gated[:, cols] * lax.rsqrt(mean + 1e-05) * gain[:, cols]).astype(BF))
    normed = jnp.concatenate(pieces, axis=1)
    part_out[...] = dot(normed, w_out[...]).astype(BF)


def readout_kernel(half, mine, other, target, gain, up, bias, down, keep_out, send_out):
    groups = up.shape[0]
    layer = mine[...].astype(F32)
    if other is not None:
        layer = layer + other[...].astype(F32)
    mean = jnp.mean(layer * layer, axis=1, keepdims=True)
    ready = (layer * lax.rsqrt(mean + 1e-05) * gain[...]).astype(BF)
    group = target[...]
    zero = jnp.zeros_like(ready)
    pre = jnp.zeros((ready.shape[0], up.shape[2]), F32)
    for g in range(groups):
        member = group == g
        pre = pre + dot(jnp.where(member, ready, zero), up[g])
        pre = pre + jnp.where(member, bias[g : g + 1, :], 0.0)
    hidden = jax.nn.gelu(pre, approximate=True).astype(BF)
    zero = jnp.zeros_like(hidden)
    out = jnp.zeros((ready.shape[0], down.shape[2]), F32)
    for g in range(groups):
        out = out + dot(jnp.where(group == g, hidden, zero), down[g])
    out = out.astype(BF)
    if send_out is None:
        keep_out[...] = out
    else:
        width = out.shape[1] // 2
        low = half[0] == 0
        keep_out[...] = jnp.where(low, out[:, :width], out[:, width:])
        send_out[...] = jnp.where(low, out[:, width:], out[:, :width])


def single_readout_kernel(mine, target, gain, up, bias, down, keep_out):
    readout_kernel(None, mine, None, target, gain, up, bias, down, keep_out, None)


def whole_block(a):
    return pl.BlockSpec(a.shape, lambda *_: (0,) * a.ndim)


def row_block(a, rows=ROWS):
    return pl.BlockSpec((rows,) + a.shape[1:], lambda i, *_: (i,) + (0,) * (a.ndim - 1))


def params():
    return pltpu.CompilerParams(vmem_limit_bytes=VMEM_BYTES, dimension_semantics=("arbitrary",))


def cost(flops, moved):
    return pl.CostEstimate(flops=int(flops), bytes_accessed=int(moved), transcendentals=0)


def split_state(packed, nstate):
    f = packed.astype(F32)
    return f[nstate : nstate + 1] + f[nstate + 1 : nstate + 2], f[:nstate]


def entering(packed, nstate):
    n_tm, n_sub = lax.axis_size("tm"), lax.axis_size("sub")
    sub = lax.axis_index("sub")
    channels = packed.shape[1]
    width = channels // n_sub
    swap = [(0, 1), (1, 0)]
    other = lax.ppermute(packed, "sub", swap)
    d_mine, s_mine = split_state(packed, nstate)
    d_other, s_other = split_state(other, nstate)
    early = sub == 0
    d_late = jnp.where(early, d_other, d_mine)
    s_late = jnp.where(early, s_other, s_mine)
    s_early = jnp.where(early, s_mine, s_other)
    d_chip = d_mine * d_other
    s_chip = d_late * s_early + s_late
    high = d_chip.astype(BF)
    low = (d_chip - high.astype(F32)).astype(BF)
    pad = jnp.zeros((14, channels), BF)
    chip = jnp.concatenate([s_chip.astype(BF), high, low, pad], axis=0)
    part = jnp.where(early, chip[:, :width], chip[:, width:])
    carry = jnp.zeros((nstate, width), F32)
    decay = jnp.ones((1, width), F32)
    for hop in range(1, n_tm):
        got = lax.ppermute(part, "tm", [(i, i + hop) for i in range(n_tm - hop)])
        d_got, s_got = split_state(got, nstate)
        carry = carry + decay * s_got
        decay = decay * d_got
    mine = carry.astype(BF)
    theirs = lax.ppermute(mine, "sub", swap)
    full = jnp.where(
        early,
        jnp.concatenate([mine, theirs], axis=1),
        jnp.concatenate([theirs, mine], axis=1),
    ).astype(F32)
    return jnp.where(early, full, d_other * full + s_other).astype(BF)


def gather_weights(w_up, w_down):
    n_groups, n_sub = lax.axis_size("groups"), lax.axis_size("sub")
    if w_up.shape != w_down.shape or n_groups != 2:
        return (
            lax.all_gather(w_up, "tm", axis=0, tiled=True),
            lax.all_gather(w_down, "tm", axis=0, tiled=True),
        )
    sub = lax.axis_index("sub")
    rows = w_up.shape[1] // n_sub
    piece = jnp.where(
        lax.axis_index("groups") == 0,
        lax.dynamic_slice_in_dim(w_up[0], sub * rows, rows, 0),
        lax.dynamic_slice_in_dim(w_down[0], sub * rows, rows, 0),
    )
    both = lax.all_gather(piece, ("groups", "tm", "sub"), axis=0, tiled=True)
    both = both.reshape(2, lax.axis_size("tm"), w_up.shape[1], w_up.shape[2])
    return both[0], both[1]


def shards(
    events, w_gate, w_inner, w_bc, w_step, step_bias, log_decay, norm_gain, w_out, mix_gain,
    port, port_shard, w_up, b_up, w_down,
):
    length, model = events.shape
    head_dim = w_inner.shape[1] // w_step.shape[1]
    if w_step.shape[1] % 2:
        w_gate = jnp.pad(w_gate, ((0, 0), (0, head_dim)))
        w_inner = jnp.pad(w_inner, ((0, 0), (0, head_dim)))
        w_step = jnp.pad(w_step, ((0, 0), (0, 1)))
        step_bias = jnp.pad(step_bias, (0, 1))
        log_decay = jnp.pad(log_decay, ((0, 1), (0, 0)))
        norm_gain = jnp.pad(norm_gain, (0, head_dim))
        w_out = jnp.pad(w_out, ((0, head_dim), (0, 0)))
    heads, channels = w_step.shape[1], w_inner.shape[1]
    nstate = w_bc.shape[1] // 2
    steps = length // ROWS
    n_mp = lax.axis_size("mp")

    bias_all = lax.all_gather(b_up, "tm", axis=0, tiled=True)
    up_all, down_all = gather_weights(w_up, w_down)

    decay_spec = pl.BlockSpec((heads, ROWS), lambda i: (0, i))
    start_spec = pl.BlockSpec((ROWS // SCAN, nstate, channels), lambda i: (i, 0, 0))
    sds = jax.ShapeDtypeStruct
    bias2 = step_bias[None, :]
    x_s, bc_s = sds((length, channels), BF), sds((length, 2 * nstate), BF)
    run_s, start_s = sds((length, heads), F32), sds((length // SCAN, nstate, channels), BF)
    end_s = sds((nstate + 16, channels), BF)
    x, bc, run, start, end = pl.pallas_call(
        project_kernel,
        grid=(steps,),
        in_specs=[row_block(events), whole_block(w_inner), whole_block(w_bc), whole_block(w_step),
                  whole_block(bias2), decay_spec],
        out_specs=[row_block(x_s), row_block(bc_s), row_block(run_s), start_spec, whole_block(end_s)],
        out_shape=[x_s, bc_s, run_s, start_s, end_s],
        scratch_shapes=[pltpu.VMEM((nstate, channels), F32), pltpu.VMEM((1, heads), F32)],
        compiler_params=params(),
        cost_estimate=cost(2 * length * model * (channels + 256), 8e6),
        name="project",
    )(events, w_inner, w_bc, w_step, bias2, log_decay)

    carry = entering(end, nstate)

    y_s = sds((length, channels), F32)
    y, gate = pl.pallas_call(
        within_kernel,
        grid=(steps,),
        in_specs=[row_block(events), whole_block(w_gate), row_block(x), row_block(bc), decay_spec,
                  start_spec],
        out_specs=[row_block(y_s), row_block(x_s)],
        out_shape=[y_s, x_s],
        compiler_params=params(),
        cost_estimate=cost(8 * length * model * channels, 12e6),
        name="within",
    )(events, w_gate, x, bc, log_decay, start)

    port_table = port[:, None] == jnp.arange(port_shard.shape[0])[None, :]
    target = jnp.sum(jnp.where(port_table, port_shard[None, :], 0), axis=1, keepdims=True)

    rows = length // CHUNKS
    gain_row = norm_gain[None, :]
    mix_row = mix_gain[None, :]
    part_s = sds((rows, model), BF)
    half = lax.axis_index("mp").astype(jnp.int32).reshape(1)

    def offset(a, c):
        per = rows // ROWS
        return pl.BlockSpec(
            (ROWS,) + a.shape[1:], lambda i: (c * per + i,) + (0,) * (a.ndim - 1)
        )

    parts, others = [], []
    for c in range(CHUNKS):
        part = pl.pallas_call(
            out_kernel,
            grid=(rows // ROWS,),
            in_specs=[offset(y, c), offset(gate, c), offset(bc, c), offset(run, c), whole_block(carry),
                      whole_block(gain_row), whole_block(w_out)],
            out_specs=row_block(part_s),
            out_shape=part_s,
            compiler_params=params(),
            cost_estimate=cost(3 * rows * model * channels, 4e6),
            name="outproj",
        )(y, gate, bc, run, carry, gain_row, w_out)
        parts.append(part)
        if n_mp == 2:
            others.append(lax.ppermute(part, "mp", [(0, 1), (1, 0)]))

    results = []
    read_cost = cost(4 * rows * model * up_all.shape[2] * up_all.shape[0], 12e6)
    for c in range(CHUNKS):
        if n_mp == 2:
            half_s = sds((rows, model // 2), BF)
            keep, send = pl.pallas_call(
                readout_kernel,
                grid=(rows // ROWS,),
                in_specs=[pl.BlockSpec(memory_space=pltpu.SMEM), row_block(part_s), row_block(part_s),
                          offset(target, c), whole_block(mix_row), whole_block(up_all),
                          whole_block(bias_all), whole_block(down_all)],
                out_specs=[row_block(half_s), row_block(half_s)],
                out_shape=[half_s, half_s],
                compiler_params=params(),
                cost_estimate=read_cost,
                name="readout",
            )(half, parts[c], others[c], target, mix_row, up_all, bias_all, down_all)
            got = lax.ppermute(send, "mp", [(0, 1), (1, 0)])
            results.append((keep.astype(F32) + got.astype(F32)).astype(BF))
        else:
            layer = lax.psum(parts[c], "mp")
            out = pl.pallas_call(
                single_readout_kernel,
                grid=(rows // ROWS,),
                in_specs=[row_block(part_s), offset(target, c), whole_block(mix_row),
                          whole_block(up_all), whole_block(bias_all), whole_block(down_all)],
                out_specs=row_block(part_s),
                out_shape=part_s,
                compiler_params=params(),
                cost_estimate=read_cost,
                name="readout",
            )(layer, target, mix_row, up_all, bias_all, down_all)
            results.append(lax.psum_scatter(out, "mp", scatter_dimension=1, tiled=True))
    return jnp.concatenate(results, axis=0)


def solution(mesh):
    in_specs = (
        P(("groups", "tm", "sub"), None),
        P(None, "mp"),
        P(None, "mp"),
        P(),
        P(None, "mp"),
        P("mp"),
        P("mp", ("groups", "tm", "sub")),
        P("mp"),
        P("mp", None),
        P(),
        P(("groups", "tm", "sub")),
        P("groups"),
        P("tm", None, "mp"),
        P("tm", "mp"),
        P("tm", "mp", None),
    )
    out_specs = P(("groups", "tm", "sub"), "mp")
    return jax.shard_map(shards, mesh=mesh, in_specs=in_specs, out_specs=out_specs, check_vma=False)
```
